128 devices in a mesh: seq: 16 (over y, x), exp: 8 (over z, core).
Axes of the slice: x: 4, y: 4, z: 4, core: 2. Of those that a mesh axis runs over, the one named last changes fastest.
Arguments:
- queries: bfloat16 [512, 64, 576], P(('seq', 'exp')), may hold values from -68 to 68
- own_latent: bfloat16 [512, 576], P(('seq', 'exp')), may hold values from -4 to 4
- snapshots: bfloat16 [2, 8192, 576], P(None, 'seq'), may hold values from -12 to 12
- leaf_snapshot: int32 [512], P(('seq', 'exp')), may hold values from 0 to 1
- moe_input: bfloat16 [512, 7168], P(('seq', 'exp')), may hold values from -6 to 6
- expert_ids: int32 [512, 8], P(('seq', 'exp')), may hold values from 0 to 7, all different within a row; in each aligned block of 4 rows (0 to 3, 4 to 7, ...) at most 4 rows name the same one
- gate_weights: float32 [512, 8], P(('seq', 'exp')), may hold values from 0.05 to 0.5
- w_gate: bfloat16 [8, 7168, 2048], P('exp', None, 'seq'), may hold values from -0.0625 to 0.0625
- w_up: bfloat16 [8, 7168, 2048], P('exp', None, 'seq'), may hold values from -0.0625 to 0.0625
- w_down: bfloat16 [8, 2048, 7168], P('exp', 'seq'), may hold values from -0.125 to 0.125
Outputs:
- attn_latent: bfloat16 [512, 64, 512], P(('seq', 'exp'))
- moe_output: bfloat16 [512, 7168], P(('seq', 'exp'))
The draws below stay inside these ranges and needn't reach their ends.
Inputs may be any that keep to these rules, and one draw needn't show every extreme that they name: `expert_ids`: each row names 8 different experts; among the 4 rows of one device, no expert is named more than 4 times.
All inputs are finite; a program needn't handle non-finite values.
Results may differ from the reference program's by a relative error of at most 0.02.
Values may be sent and summed in bfloat16 or wider, within the bound.
No kernel may reach another device: no remote copies, remote signals or barrier semaphores. Data moves between devices by JAX's collectives and lax.ppermute only.
A program may use at most 192 MiB of HBM per device.

```python
import math
import jax
import jax.numpy as jnp
import numpy as np
from jax import lax

D = 7168
FF = 2048
LAT = 512
TOP = 8
HEADS = 64
KDIM = 576
FF_DEV = 128
EXPERTS = 8
LEAF_DEV = 4
CAP = 4
POS_DEV = 512
SNAPS = 2
SNAP_LEN = 8192
LEAVES = 512


qk_scale = 192.0 ** (-0.5)


def own_values(key, rope_factor):
    base = jax.random.truncated_normal(jax.random.fold_in(key, 7), -4.0, 4.0, (LEAVES, KDIM), jnp.float32)
    factor = jnp.where(jnp.arange(KDIM) < LAT, 1.0, rope_factor)
    return base * factor[None, :]


def own_share():
    return (math.log(SNAP_LEN) + 1.0) / (qk_scale * KDIM)


def draw_own_latent(key, part):
    values = own_values(key, 1.0)
    return values.astype(jnp.bfloat16)


def draw_queries(key, part):
    noise = jax.random.truncated_normal(jax.random.fold_in(key, 13), -4.0, 4.0, (LEAVES, HEADS, KDIM), jnp.float32)
    mixed = 0.5 * noise + own_share() * own_values(key, 1.0)[:, None, :]
    return mixed.astype(jnp.bfloat16)


def draw_snapshots(key, part):
    log_scale = jax.random.uniform(jax.random.fold_in(key, 17), (SNAPS, SNAP_LEN, 1), jnp.float32, math.log(0.5), math.log(3.0))
    row_scale = jnp.exp(log_scale)
    values = jax.random.truncated_normal(jax.random.fold_in(key, 19), -4.0, 4.0, (SNAPS, SNAP_LEN, KDIM), jnp.float32)
    values = values * row_scale
    return values.astype(jnp.bfloat16)


def touch_ends(result, stream_key, least, high):
    place = [jax.random.randint(jax.random.fold_in(stream_key, axis), (), 0, length) for axis, length in enumerate(result.shape)]
    main_axis = result.shape.index(max(result.shape))
    beside = place[:main_axis] + [(place[main_axis] + 1) % result.shape[main_axis]] + place[main_axis + 1:]
    return result.at[tuple(place)].set(least).at[tuple(beside)].set(high)


def levels(key, shape, split, least, top_value):
    def one(dim, shards_of):
        heights = jax.random.uniform(jax.random.fold_in(jax.random.fold_in(key, 6), dim), (shards_of,), jnp.float32, least / len(split), top_value / len(split))
        return jnp.repeat(jnp.exp(heights), shape[dim] // shards_of).reshape((-1,) + (1,) * (len(shape) - dim - 1))

    gain = one(*split[0])
    for cut in split[1:]:
        gain = gain * one(*cut)
    return gain


def routed_block(key, own, number, rows, count, top, reach, slope):
    sequence = jax.random.permutation(key, count)
    crowded, usual = shares(count, rows * top, reach, slope, True), shares(count, rows * top, reach, slope, False)
    places = jnp.arange(count)

    def named(tallies, offset_by):
        used = int((tallies > 0).sum())
        fixed = max(1, used // 4)
        shifted = fixed + (places - fixed + offset_by * (used - fixed)) % max(1, count - fixed)
        return jnp.zeros((count,), jnp.int32).at[sequence[jnp.where(places < fixed, places, shifted)]].set(jnp.asarray(tallies, jnp.int32))

    tallies = jnp.where(number % 4 == 0, named(crowded, number // 4), named(usual, number - number // 4 - 1))
    mixed = jax.random.permutation(jax.random.fold_in(own, 3), count)
    donor, receiver = mixed[0:count // 2 * 2:2], mixed[1:count // 2 * 2:2]
    slack = jnp.minimum(tallies[donor] - 1, reach - tallies[receiver]) // 2
    slack = jnp.where((donor == sequence[0]) | (receiver == sequence[0]) | (tallies[receiver] == 0), 0, jnp.maximum(slack, 0))
    shifted = jax.random.randint(jax.random.fold_in(own, 4), (count // 2,), 0, 1 << 20) % (slack + 1)
    tallies = tallies.at[donor].add(-shifted).at[receiver].add(shifted)
    items = jnp.searchsorted(jnp.cumsum(tallies), jnp.arange(rows * top), side="right").astype(jnp.int32)
    grid = items.reshape(top, rows).T
    grid = grid[jax.random.permutation(jax.random.fold_in(own, 1), rows)]
    offset_by = jax.random.randint(jax.random.fold_in(own, 2), (rows, 1), 0, top)
    return jnp.take_along_axis(grid, (jnp.arange(top)[None, :] + offset_by) % top, axis=1)


def shares(count, total, limit, lean, full):
    portions = [(1 << 20) // math.isqrt(standing ** lean) + 1 for standing in range(1, count + 1)]
    largest = limit if full else min(limit, max(-(-total // count), total * portions[0] // sum(portions)))
    least = 1 if total - largest >= count - 1 else 0
    counts, rest = [largest] + [least] * (count - 1), total - largest - least * (count - 1)
    while rest > 0:
        movable = [i for i in range(1, count) if counts[i] < largest] or [i for i in range(1, count) if counts[i] < limit]
        mass, left = sum([portions[i] for i in movable]), rest
        for i in movable:
            extra = min(limit - counts[i], max(1, left * portions[i] // mass), rest)
            counts[i] = counts[i] + extra
            rest = rest - extra
    return np.array(counts)


def scatter_about(key, extent, scale, bound, shards=(), held_as=jnp.bfloat16):
    result = jax.random.normal(key, extent, jnp.float32) * scale
    if len(shards) > 0:
        result = levels(key, extent, shards, -0.22, 0.18) * result
    return jnp.clip(result, min=-bound, max=bound).astype(held_as)


def setup_inputs(seed: int = 0) -> dict:
    splits = jax.random.split(jax.random.key(seed), 11)
    queries = draw_queries(jax.random.fold_in(splits[10], 71), 0)
    own_latent = draw_own_latent(jax.random.fold_in(splits[10], 71), 0)
    snapshots = draw_snapshots(jax.random.fold_in(splits[10], 71), 0)
    leaf_snapshot = touch_ends(jax.random.randint(splits[3], (LEAVES,), 0, SNAPS), jax.random.fold_in(splits[3], 1), 0, SNAPS - 1).astype(jnp.int32)
    moe_input = scatter_about(splits[4], (LEAVES, D), 1.0, 6.0, ((0, 128),))
    expert_ids_keys = jax.random.split(jax.random.fold_in(splits[5], 1), LEAVES // LEAF_DEV)
    expert_ids_turns = jax.random.permutation(jax.random.fold_in(splits[5], 3), LEAVES // LEAF_DEV)
    expert_ids = jax.vmap(lambda own, number: routed_block(jax.random.fold_in(splits[5], 2), own, number, LEAF_DEV, EXPERTS, TOP, CAP, 2))(expert_ids_keys, expert_ids_turns).reshape((LEAVES, TOP))
    gate_weights = jnp.clip(jnp.exp(math.log(0.5) - 2.3025851 * jax.random.uniform(splits[6], (LEAVES, TOP), jnp.float32) ** levels(splits[6], (LEAVES, TOP), ((0, 128),), -0.2, 0.2)), 0.05, 0.5)
    w_gate = scatter_about(splits[7], (EXPERTS, D, FF), D ** -0.5, 0.0625, ((0, 8), (2, 16)))
    w_up = scatter_about(splits[8], (EXPERTS, D, FF), D ** -0.5, 0.0625, ((0, 8), (2, 16)))
    w_down = scatter_about(splits[9], (EXPERTS, FF, D), FF ** -0.5, 0.125, ((0, 8), (1, 16)))
    return dict(queries=queries, own_latent=own_latent, snapshots=snapshots, leaf_snapshot=leaf_snapshot, moe_input=moe_input, expert_ids=expert_ids, gate_weights=gate_weights, w_gate=w_gate, w_up=w_up, w_down=w_down)


qk_scale = 192.0 ** -0.5


def attend_leaf(query_heads, snapshot_rows, own_key):
    scores = qk_scale * jnp.dot(query_heads, snapshot_rows.T, preferred_element_type=jnp.float32)
    own_score = qk_scale * jnp.dot(query_heads, own_key, preferred_element_type=jnp.float32)
    row_max = jnp.maximum(jnp.max(scores, axis=1), own_score)
    weights = jnp.exp(scores - row_max[:, None]).astype(jnp.bfloat16)
    block_count = SNAP_LEN // POS_DEV
    blocked = weights.reshape(HEADS, block_count, POS_DEV).astype(jnp.float32)
    mass_parts = jnp.sum(blocked, axis=2)
    mass_parts = lax.optimization_barrier(mass_parts.astype(jnp.bfloat16)).astype(jnp.float32)
    latent_blocks = snapshot_rows[:, :LAT].reshape(block_count, POS_DEV, LAT).astype(jnp.float32)
    value_parts = jnp.einsum("hbp,bpl->hbl", blocked, latent_blocks, precision=lax.Precision.HIGHEST)
    value_parts = lax.optimization_barrier(value_parts.astype(jnp.bfloat16)).astype(jnp.float32)
    own_weight = jnp.exp(own_score - row_max)
    numerator = jnp.sum(value_parts, axis=1) + own_weight[:, None] * own_key[:LAT].astype(jnp.float32)
    denominator = jnp.sum(mass_parts, axis=1) + own_weight
    return (numerator / denominator[:, None]).astype(jnp.bfloat16)


def attention(queries, own_latent, snapshots, leaf_snapshot):
    def one_leaf(packed):
        query_heads, own_key, snapshot_index = packed
        snapshot_rows = lax.dynamic_index_in_dim(snapshots, snapshot_index, 0, keepdims=False)
        return attend_leaf(query_heads, snapshot_rows, own_key)

    return lax.map(one_leaf, (queries, own_latent, leaf_snapshot))


def expert_block(packed):
    slot_rows, gate_matrix, up_matrix, down_matrix = packed
    flat_rows = slot_rows.reshape(-1, D)
    gate_proj = jnp.dot(flat_rows, gate_matrix, preferred_element_type=jnp.float32)
    up_proj = jnp.dot(flat_rows, up_matrix, preferred_element_type=jnp.float32)
    hidden = (jax.nn.silu(gate_proj) * up_proj).astype(jnp.bfloat16)
    summed = jnp.zeros((flat_rows.shape[0], D), jnp.float32)
    for slice_index in range(FF // FF_DEV):
        offset = slice_index * FF_DEV
        partial_out = jnp.dot(hidden[:, offset:offset + FF_DEV], down_matrix[offset:offset + FF_DEV], preferred_element_type=jnp.float32)
        summed = summed + lax.optimization_barrier(partial_out.astype(jnp.bfloat16)).astype(jnp.float32)
    return summed.astype(jnp.bfloat16).reshape(slot_rows.shape)


def mixture(moe_input, expert_ids, gate_weights, w_gate, w_up, w_down):
    source_count = LEAVES // LEAF_DEV
    ids_blocked = expert_ids.reshape(source_count, LEAF_DEV, TOP)
    chosen = (ids_blocked[..., None] == jnp.arange(EXPERTS, dtype=jnp.int32)).astype(jnp.int32)
    per_row = jnp.sum(chosen, axis=2).astype(jnp.int32)
    earlier = (jnp.cumsum(per_row, axis=1) - per_row).astype(jnp.int32)
    slot_rank = jnp.take_along_axis(earlier, ids_blocked, axis=2).astype(jnp.int32)
    source_index = jnp.broadcast_to(jnp.arange(source_count, dtype=jnp.int32)[:, None, None], ids_blocked.shape)
    inputs_blocked = jnp.broadcast_to(moe_input.reshape(source_count, LEAF_DEV, 1, D), (source_count, LEAF_DEV, TOP, D))
    slot_table = jnp.zeros((EXPERTS, source_count, CAP, D), jnp.bfloat16)
    slot_table = slot_table.at[ids_blocked, source_index, slot_rank].set(inputs_blocked)
    outputs = lax.map(expert_block, (slot_table, w_gate, w_up, w_down))
    picked = outputs[ids_blocked, source_index, slot_rank]
    weighted = jnp.sum(gate_weights.reshape(source_count, LEAF_DEV, TOP, 1) * picked.astype(jnp.float32), axis=2)
    return weighted.reshape(LEAVES, D).astype(jnp.bfloat16)


def reference(queries, own_latent, snapshots, leaf_snapshot, moe_input, expert_ids, gate_weights, w_gate, w_up, w_down):
    attn_latent = attention(queries, own_latent, snapshots, leaf_snapshot)
    moe_output = mixture(moe_input, expert_ids, gate_weights, w_gate, w_up, w_down)
    return (attn_latent, moe_output)
```

```python
import math

import jax
import jax.numpy as jnp
from jax import lax
from jax.experimental import pallas as pl
from jax.experimental.pallas import tpu as pltpu
from jax.sharding import PartitionSpec as P

LAT = 512
KDIM = 576
QW = 640
D = 7168
XW = D + 128
C1 = 4608
C2 = XW - C1
E1 = 3584
E2 = D - E1
KC = 1536
SCALE2 = 192.0 ** (-0.5) * math.log2(math.e)
AXES = ("seq", "exp")
bf16 = jnp.bfloat16
f32 = jnp.float32


def shift(a, axis, s):
    pairs = []
    for y in range(4):
        for x in range(4):
            for z in range(4):
                for c in range(2):
                    to = dict(y=y, x=x, z=z, c=c)
                    to[axis] = (to[axis] + s) % (2 if axis == "c" else 4)
                    src = ((y * 4 + x) * 4 + z) * 2 + c
                    dst = ((to["y"] * 4 + to["x"]) * 4 + to["z"]) * 2 + to["c"]
                    pairs.append((src, dst))
    return lax.ppermute(a, AXES, pairs)


def spread(a, axis):
    return [a] + [shift(a, axis, s) for s in (1, 2, 3)]


def fold(chunks, axis):
    got = [shift(chunks[s], axis, -s) for s in (1, 2, 3)]
    return chunks[0].astype(f32) + got[0].astype(f32) + got[1].astype(f32) + got[2].astype(f32)


def attend_kernel(core_ref, *refs):
    qs, own, near, far = refs[0:4], refs[4], refs[5:8], refs[8:11]
    outs, s_ref = refs[11:15], refs[15]
    core = core_ref[0]
    coref = core.astype(f32)
    tiles_a = [own.at[core]] + list(near)
    tiles_b = [own.at[1 - core]] + list(far)
    tiles = tiles_a + tiles_b
    lane = lax.broadcasted_iota(jnp.int32, (256, QW - LAT), 1)
    for q_ref, o_ref in zip(qs, outs):
        q = q_ref[:, 0:KDIM]
        is_a = q_ref[:, KDIM : KDIM + 1].astype(f32) == coref
        best = []
        for group in range(2):
            m = None
            for t in range(4):
                i = group * 4 + t
                s = lax.dot_general(
                    q, tiles[i][...], (((1,), (1,)), ((), ())), preferred_element_type=f32
                )
                s_ref[i] = s
                ms = jnp.max(s, axis=1, keepdims=True)
                m = ms if m is None else jnp.maximum(m, ms)
            best.append(m)
        mu = jnp.where(is_a, best[0], best[1]) * SCALE2
        hi = mu.astype(bf16).astype(f32)
        lo = (mu - hi).astype(bf16).astype(f32)
        top = hi + lo
        total = jnp.zeros((256, 1), f32)
        acc = jnp.zeros((256, LAT), f32)
        for i in range(8):
            off = jnp.where(is_a if i < 4 else jnp.logical_not(is_a), -top, -1e30)
            w = jnp.exp2(s_ref[i] * SCALE2 + off).astype(bf16)
            total = total + jnp.sum(w.astype(f32), axis=1, keepdims=True)
            acc = acc + jnp.dot(w, tiles[i][:, 0:LAT], preferred_element_type=f32)
        o_ref[:, 0:LAT] = acc.astype(bf16)
        l_hi = total.astype(bf16).astype(f32)
        l_lo = total - l_hi
        tail = jnp.where(
            lane == 0,
            hi,
            jnp.where(lane == 1, lo, jnp.where(lane == 2, l_hi, jnp.where(lane == 3, l_lo, 0.0))),
        )
        o_ref[:, LAT:QW] = tail.astype(bf16)


def attend(core, qs, own, near, far):
    vmem = pl.BlockSpec(memory_space=pltpu.VMEM)
    return pl.pallas_call(
        attend_kernel,
        out_shape=[jax.ShapeDtypeStruct((256, QW), bf16)] * 4,
        in_specs=[pl.BlockSpec(memory_space=pltpu.SMEM)] + [vmem] * 11,
        out_specs=[vmem] * 4,
        scratch_shapes=[pltpu.VMEM((8, 256, 512), f32)],
        compiler_params=pltpu.CompilerParams(vmem_limit_bytes=40 << 20),
        name="attend",
    )(core, *qs, own, *near, *far)


def merge_kernel(q_ref, lat_ref, *refs):
    parts, out_ref = refs[0:4], refs[4]
    for leaf in range(4):
        r = slice(leaf * 64, leaf * 64 + 64)
        lat = lat_ref[leaf : leaf + 1, :].astype(f32)
        own = jnp.sum(q_ref[r, 0:KDIM].astype(f32) * lat, axis=1, keepdims=True) * SCALE2
        tails = [p[r, LAT:QW].astype(f32) for p in parts]
        tops = [t[:, 0:1] + t[:, 1:2] for t in tails]
        m = own
        for t in tops:
            m = jnp.maximum(m, t)
        w = jnp.exp2(own - m)
        num = w * lat[:, 0:LAT]
        den = w
        for p, t, top in zip(parts, tails, tops):
            w = jnp.exp2(top - m)
            num = num + w * p[r, 0:LAT].astype(f32)
            den = den + w * (t[:, 2:3] + t[:, 3:4])
        out_ref[r, :] = (num / den).astype(bf16)


def merge(q, lat, parts):
    vmem = pl.BlockSpec(memory_space=pltpu.VMEM)
    return pl.pallas_call(
        merge_kernel,
        out_shape=jax.ShapeDtypeStruct((256, LAT), bf16),
        in_specs=[vmem] * 6,
        out_specs=vmem,
        name="merge",
    )(q, lat, *parts)


def expert_kernel(e_ref, *refs):
    x1, x2 = refs[0:4], refs[4:8]
    wg, wu, wd, wg2, wu2, wd2 = refs[8:14]
    outs = refs[14:22]
    x_ref, w_ref, d_ref, acc_ref, sems = refs[22:27]
    bounds = [(k, min(k + KC, C1)) for k in range(0, C1, KC)] + [(C1, D)]
    count = [0]

    def copy(src, dst):
        cp = pltpu.make_async_copy(src, dst, sems.at[count[0]])
        count[0] += 1
        cp.start()
        return cp

    steps = []
    for k0, k1 in bounds:
        cps = []
        for j, w in enumerate((wg, wu, wg2, wu2)):
            cps.append(copy(w.at[k0:k1, :], w_ref.at[k0:k1, j * 128 : j * 128 + 128]))
        if k0 < C1:
            for z in range(4):
                cps.append(copy(x1[z].at[:, k0:k1], x_ref.at[z * 64 : z * 64 + 64, k0:k1]))
        else:
            for y in range(4):
                for z in range(4):
                    cps.append(
                        copy(
                            x2[y].at[z * 16 : z * 16 + 16, :],
                            x_ref.at[z * 64 + y * 16 : z * 64 + y * 16 + 16, C1:XW],
                        )
                    )
        steps.append(cps)
    down = [copy(wd, d_ref.at[0:128, :]), copy(wd2, d_ref.at[128:256, :])]
    for i, (k0, k1) in enumerate(bounds):
        for cp in steps[i]:
            cp.wait()
        part = jnp.dot(x_ref[:, k0:k1], w_ref[k0:k1, :], preferred_element_type=f32)
        if i == 0:
            acc_ref[...] = part
        else:
            acc_ref[...] += part
    gates = x_ref[:, D:XW].astype(f32)
    lane = lax.broadcasted_iota(jnp.int32, (256, 128), 1)
    halves = []
    for j in range(2):
        e = e_ref[j]
        pick = jnp.logical_or(lane == e, lane == e + 8)
        weight = jnp.sum(jnp.where(pick, gates, 0.0), axis=1, keepdims=True)
        g = acc_ref[:, j * 256 : j * 256 + 128]
        u = acc_ref[:, j * 256 + 128 : j * 256 + 256]
        halves.append((g / (1.0 + jnp.exp(-g)) * u * weight).astype(bf16))
    hidden = jnp.concatenate(halves, axis=1)
    row = lax.broadcasted_iota(jnp.int32, (256, 256), 0)
    col = lax.broadcasted_iota(jnp.int32, (256, 256), 1)
    i0 = row & 3
    b1 = (row >> 2) & 3
    b2 = (row >> 4) & 3
    b3 = (row >> 6) & 3
    want1 = b3 * 64 + b1 * 16 + b2 * 4 + i0
    want2 = b2 * 64 + b1 * 16 + b3 * 4 + i0
    for cp in down:
        cp.wait()
    for part, (want, base, width) in enumerate(((want1, 0, E1), (want2, E1, E2))):
        place = jnp.where(col == want, 1.0, 0.0).astype(bf16)
        h = jnp.dot(place, hidden, preferred_element_type=f32).astype(bf16)
        for n in range(0, width, 512):
            y = jnp.dot(h, d_ref[:, base + n : base + n + 512], preferred_element_type=f32).astype(
                bf16
            )
            for s in range(4):
                outs[part * 4 + s][:, n : n + 512] = y[s * 64 : s * 64 + 64, :]


def experts(e, x1, x2, weights):
    vmem = pl.BlockSpec(memory_space=pltpu.VMEM)
    hbm = pl.BlockSpec(memory_space=pl.ANY)
    return pl.pallas_call(
        expert_kernel,
        out_shape=[jax.ShapeDtypeStruct((64, E1), bf16)] * 4
        + [jax.ShapeDtypeStruct((64, E2), bf16)] * 4,
        in_specs=[pl.BlockSpec(memory_space=pltpu.SMEM)] + [hbm] * 14,
        out_specs=[vmem] * 8,
        scratch_shapes=[
            pltpu.VMEM((256, XW), bf16),
            pltpu.VMEM((D, 512), bf16),
            pltpu.VMEM((256, D), bf16),
            pltpu.VMEM((256, 512), f32),
            pltpu.SemaphoreType.DMA((64,)),
        ],
        compiler_params=pltpu.CompilerParams(vmem_limit_bytes=48 << 20),
        name="experts",
    )(e, *x1, *x2, *weights)


def body(
    queries,
    own_latent,
    snapshots,
    leaf_snapshot,
    moe_input,
    expert_ids,
    gate_weights,
    w_gate,
    w_up,
    w_down,
):
    place = lax.axis_index("exp").astype(jnp.int32)
    core = place & 1

    hit = (expert_ids[:, :, None] == jnp.arange(8, dtype=jnp.int32)).astype(f32)
    gate = jnp.sum(gate_weights[:, :, None] * hit, axis=1)
    high = lax.reduce_precision(gate, 8, 7)
    tail = jnp.concatenate([high, gate - high, jnp.zeros((4, 112), f32)], axis=1).astype(bf16)
    row = jnp.concatenate([moe_input, tail], axis=1)
    rows = jnp.concatenate(spread(row, "x"), axis=0)
    rows1 = jnp.concatenate(spread(rows[:, :C1], "y"), axis=0)
    rows2 = jnp.concatenate(spread(rows[:, C1:], "z"), axis=0)
    x1 = spread(rows1, "z")
    x2 = spread(rows2, "y")
    weights = [w_gate[0], w_up[0], w_down[0]]
    weights = weights + [shift(w, "c", 1) for w in weights]

    choice = jnp.broadcast_to(leaf_snapshot.astype(bf16)[:, None, None], (4, 64, QW - KDIM))
    query = jnp.concatenate([queries, choice], axis=2).reshape(256, QW)
    query_all = spread(query, "y")
    half = lax.dynamic_index_in_dim(snapshots, core, 0, keepdims=False)
    near = [shift(half, "x", s) for s in (1, 2, 3)]
    far = [shift(a, "c", 1) for a in near]

    parts = attend(core[None], query_all, snapshots, near, far)
    back = [parts[0]] + [shift(parts[s], "y", -s) for s in (1, 2, 3)]
    attn = merge(query, own_latent, back).reshape(4, 64, LAT)

    out = experts(jnp.stack([place, place ^ 1]), x1, x2, weights)
    a1 = fold(out[0:4], "z").astype(bf16)
    a2 = fold(out[4:8], "x").astype(bf16)
    b1 = fold([a1[s * 16 : s * 16 + 16] for s in range(4)], "x").astype(bf16)
    b2 = fold([a2[s * 16 : s * 16 + 16] for s in range(4)], "z").astype(bf16)
    b = jnp.concatenate([b1, b2], axis=1)
    moe = fold([b[s * 4 : s * 4 + 4] for s in range(4)], "y").astype(bf16)
    return attn, moe


def solution(mesh):
    in_specs = (
        P(AXES, None, None),
        P(AXES, None),
        P(None, "seq", None),
        P(AXES),
        P(AXES, None),
        P(AXES, None),
        P(AXES, None),
        P("exp", None, "seq"),
        P("exp", None, "seq"),
        P("exp", "seq", None),
    )
    out_specs = (P(AXES, None, None), P(AXES, None))
    return jax.shard_map(body, mesh=mesh, in_specs=in_specs, out_specs=out_specs, check_vma=False)
```

```python
import math

import jax
import jax.numpy as jnp
from jax import lax
from jax.experimental import pallas as pl
from jax.experimental.pallas import tpu as pltpu
from jax.sharding import PartitionSpec as P

LAT = 512
KDIM = 576
QW = 640
D = 7168
XW = D + 128
KC = 2560
SCALE2 = 192.0 ** (-0.5) * math.log2(math.e)
AXES = ("seq", "exp")
GROUPS_X = [[4 * y + x for x in range(4)] for y in range(4)]
bf16 = jnp.bfloat16
f32 = jnp.float32


def shift(a, axis, s):
    pairs = []
    for y in range(4):
        for x in range(4):
            for z in range(4):
                for c in range(2):
                    to = dict(y=y, x=x, z=z, c=c)
                    to[axis] = (to[axis] + s) % (2 if axis == "c" else 4)
                    src = ((y * 4 + x) * 4 + z) * 2 + c
                    dst = ((to["y"] * 4 + to["x"]) * 4 + to["z"]) * 2 + to["c"]
                    pairs.append((src, dst))
    return lax.ppermute(a, AXES, pairs)


def gather(a, axis, groups):
    wide = jnp.broadcast_to(a, (len(groups[0]),) + a.shape[1:])
    return lax.all_to_all(wide, axis, 0, 0, tiled=True, axis_index_groups=groups)


def after(*arrays):
    return lax.optimization_barrier(arrays)


def add(*parts):
    out = parts[0].astype(f32)
    for p in parts[1:]:
        out = out + p.astype(f32)
    return out.astype(bf16)


def in_hbm(*arrays):
    return [pltpu.with_memory_space_constraint(a, pltpu.HBM) for a in arrays]


def attend_kernel(core_ref, *refs):
    qs, near, far, outs = refs[0:2], refs[2], refs[3], refs[4:6]
    q_ref, k_ref, s_ref, o_ref, sems = refs[6:11]
    coref = core_ref[0].astype(f32)
    cps = []

    def load(src, dst):
        cps.append(pltpu.make_async_copy(src, dst, sems.at[len(cps) + 2]))

    load(qs[0], q_ref.at[0])
    load(qs[1], q_ref.at[1])
    load(near, k_ref.at[0])
    load(far, k_ref.at[1])
    for cp in cps:
        cp.start()
    for cp in cps:
        cp.wait()
    lane = lax.broadcasted_iota(jnp.int32, (256, QW - LAT), 1)
    stores = []
    for step in range(2):
        q = q_ref[step, :, 0:KDIM]
        is_a = q_ref[step, :, KDIM : KDIM + 1].astype(f32) == coref
        best = []
        for g in range(2):
            m = None
            for t in range(4):
                s = jnp.dot(q, k_ref[g, t], preferred_element_type=f32)
                s_ref[g * 4 + t] = s
                ms = jnp.max(s, axis=1, keepdims=True)
                m = ms if m is None else jnp.maximum(m, ms)
            best.append(m)
        mu = jnp.where(is_a, best[0], best[1]) * SCALE2
        hi = mu.astype(bf16).astype(f32)
        lo = (mu - hi).astype(bf16).astype(f32)
        top = hi + lo
        total = jnp.zeros((256, 1), f32)
        acc = jnp.zeros((256, LAT), f32)
        for g in range(2):
            off = jnp.where(is_a if g == 0 else jnp.logical_not(is_a), -top, -1e30)
            for t in range(4):
                w = jnp.exp2(s_ref[g * 4 + t] * SCALE2 + off).astype(bf16)
                total = total + jnp.sum(w.astype(f32), axis=1, keepdims=True)
                acc = acc + lax.dot_general(
                    w,
                    k_ref[g, t, 0:LAT, :],
                    (((1,), (1,)), ((), ())),
                    preferred_element_type=f32,
                )
        o_ref[step, :, 0:LAT] = acc.astype(bf16)
        l_hi = total.astype(bf16).astype(f32)
        l_lo = total - l_hi
        tail = jnp.where(
            lane == 0,
            hi,
            jnp.where(lane == 1, lo, jnp.where(lane == 2, l_hi, jnp.where(lane == 3, l_lo, 0.0))),
        )
        o_ref[step, :, LAT:QW] = tail.astype(bf16)
        cp = pltpu.make_async_copy(o_ref.at[step], outs[step], sems.at[step])
        cp.start()
        stores.append(cp)
    for cp in stores:
        cp.wait()


def attend(core, qs, near, far):
    hbm = pl.BlockSpec(memory_space=pltpu.HBM)
    return pl.pallas_call(
        attend_kernel,
        out_shape=[pltpu.HBM((256, QW), bf16)] * 2,
        in_specs=[pl.BlockSpec(memory_space=pltpu.SMEM)] + [hbm] * 4,
        out_specs=[hbm] * 2,
        scratch_shapes=[
            pltpu.VMEM((2, 256, QW), bf16),
            pltpu.VMEM((2, 4, KDIM, 512), bf16),
            pltpu.VMEM((8, 256, 512), f32),
            pltpu.VMEM((2, 256, QW), bf16),
            pltpu.SemaphoreType.DMA((6,)),
        ],
        compiler_params=pltpu.CompilerParams(vmem_limit_bytes=40 << 20),
        cost_estimate=pl.CostEstimate(
            flops=4_500_000_000, transcendentals=2_000_000, bytes_accessed=6_000_000
        ),
        name="attend",
    )(core, *in_hbm(*qs, near, far))


def merge_kernel(q_ref, lat_ref, *refs):
    parts, out_ref = refs[0:4], refs[4]
    for leaf in range(4):
        r = slice(leaf * 64, leaf * 64 + 64)
        lat = lat_ref[leaf : leaf + 1, :].astype(f32)
        own = jnp.sum(q_ref[r, 0:KDIM].astype(f32) * lat, axis=1, keepdims=True) * SCALE2
        tails = [p[r, LAT:QW].astype(f32) for p in parts]
        tops = [t[:, 0:1] + t[:, 1:2] for t in tails]
        m = own
        for t in tops:
            m = jnp.maximum(m, t)
        w = jnp.exp2(own - m)
        num = w * lat[:, 0:LAT]
        den = w
        for p, t, top in zip(parts, tails, tops):
            w = jnp.exp2(top - m)
            num = num + w * p[r, 0:LAT].astype(f32)
            den = den + w * (t[:, 2:3] + t[:, 3:4])
        out_ref[r, :] = (num / den).astype(bf16)


def merge(q, lat, parts):
    vmem = pl.BlockSpec(memory_space=pltpu.VMEM)
    return pl.pallas_call(
        merge_kernel,
        out_shape=jax.ShapeDtypeStruct((256, LAT), bf16),
        in_specs=[vmem] * 6,
        out_specs=vmem,
        name="merge",
    )(q, lat, *parts)


def expert_kernel(e_ref, *refs):
    xs, (wg, wu, wd, wg2, wu2, wd2), outs = refs[0:5], refs[5:11], refs[11:16]
    x_ref, w_ref, d_ref, acc_ref, o_ref, sems = refs[16:22]
    bounds = [(k, min(k + KC, D)) for k in range(0, D, KC)]
    count = [0]

    def copy(src, dst):
        cp = pltpu.make_async_copy(src, dst, sems.at[count[0]])
        count[0] += 1
        cp.start()
        return cp

    steps = []
    for k0, k1 in bounds:
        cps = []
        for j, w in enumerate((wg, wu, wg2, wu2)):
            cps.append(copy(w.at[k0:k1, :], w_ref.at[k0:k1, j * 128 : j * 128 + 128]))
        end = XW if k1 == D else k1
        r = 0
        for x in xs:
            cps.append(copy(x.at[:, k0:end], x_ref.at[r : r + x.shape[0], k0:end]))
            r += x.shape[0]
        steps.append(cps)
    down = [copy(wd, d_ref.at[0:128, :]), copy(wd2, d_ref.at[128:256, :])]
    for i, (k0, k1) in enumerate(bounds):
        for cp in steps[i]:
            cp.wait()
        part = jnp.dot(x_ref[:, k0:k1], w_ref[k0:k1, :], preferred_element_type=f32)
        if i == 0:
            acc_ref[...] = part
        else:
            acc_ref[...] += part
    gates = x_ref[:, D:XW].astype(f32)
    lane = lax.broadcasted_iota(jnp.int32, (256, 128), 1)
    halves = []
    for j in range(2):
        e = e_ref[j]
        pick = jnp.logical_or(lane == e, lane == e + 8)
        weight = jnp.sum(jnp.where(pick, gates, 0.0), axis=1, keepdims=True)
        g = acc_ref[:, j * 256 : j * 256 + 128]
        u = acc_ref[:, j * 256 + 128 : j * 256 + 256]
        halves.append((g / (1.0 + jnp.exp(-g)) * u * weight).astype(bf16))
    hidden = jnp.concatenate(halves, axis=1)
    for cp in down:
        cp.wait()
    stores = []
    for n in range(0, D, 1024):
        y = jnp.dot(hidden, d_ref[:, n : n + 1024], preferred_element_type=f32)
        o_ref[:, n : n + 1024] = y.astype(bf16)
        r = 0
        for out in outs:
            stores.append(
                copy(o_ref.at[r : r + out.shape[0], n : n + 1024], out.at[:, n : n + 1024])
            )
            r += out.shape[0]
    for cp in stores:
        cp.wait()


def experts(e, xs, weights):
    hbm = pl.BlockSpec(memory_space=pltpu.HBM)
    return pl.pallas_call(
        expert_kernel,
        out_shape=[pltpu.HBM((n, D), bf16) for n in (64, 64, 32, 32, 64)],
        in_specs=[pl.BlockSpec(memory_space=pltpu.SMEM)] + [hbm] * 11,
        out_specs=[hbm] * 5,
        scratch_shapes=[
            pltpu.VMEM((256, XW), bf16),
            pltpu.VMEM((D, 512), bf16),
            pltpu.VMEM((256, D), bf16),
            pltpu.VMEM((256, 512), f32),
            pltpu.VMEM((256, D), bf16),
            pltpu.SemaphoreType.DMA((72,)),
        ],
        compiler_params=pltpu.CompilerParams(vmem_limit_bytes=48 << 20),
        cost_estimate=pl.CostEstimate(
            flops=3_000_000_000, transcendentals=65_536, bytes_accessed=18_000_000
        ),
        name="experts",
    )(e, *in_hbm(*xs, *weights))


def body(
    queries,
    own_latent,
    snapshots,
    leaf_snapshot,
    moe_input,
    expert_ids,
    gate_weights,
    w_gate,
    w_up,
    w_down,
):
    place = lax.axis_index("exp").astype(jnp.int32)
    core = place & 1

    hit = (expert_ids[:, :, None] == jnp.arange(8, dtype=jnp.int32)).astype(f32)
    gate = jnp.sum(gate_weights[:, :, None] * hit, axis=1)
    high = lax.reduce_precision(gate, 8, 7)
    tail = jnp.concatenate([high, gate - high, jnp.zeros((4, 112), f32)], axis=1).astype(bf16)
    row = jnp.concatenate([moe_input, tail], axis=1)
    rows = lax.all_to_all(
        jnp.broadcast_to(row[None], (16, 4, XW)), "seq", 0, 0, tiled=True
    ).reshape(64, XW)
    weights = [w_gate[0], w_up[0], w_down[0]]
    other = [shift(w, "c", 1) for w in weights]

    choice = jnp.broadcast_to(leaf_snapshot.astype(bf16)[:, None, None], (4, 64, QW - KDIM))
    query = jnp.concatenate([queries, choice], axis=2).reshape(256, QW)
    half = lax.dynamic_index_in_dim(jnp.transpose(snapshots, (0, 2, 1)), core, 0, keepdims=True)
    rows, half, query, *other = after(rows, half, query, *other)
    weights = weights + other

    z1, z3 = shift(rows, "z", 1), shift(rows, "z", 3)
    near = gather(half, "seq", GROUPS_X)
    q1, q3, q2 = shift(query, "y", 1), shift(query, "y", 3), shift(query, "y", 2)
    z1, z3, q1, q3, q2 = after(z1, z3, q1, q3, q2)
    xs = [rows, z1, shift(z1[:32], "z", 1), shift(z3[32:], "z", 3), z3]
    xs, near, q1, q2, q3 = after(xs, near, q1, q2, q3)
    far = shift(near, "c", 1)

    out0, out1, low, high, out3 = experts(jnp.stack([place, place ^ 1]), xs, weights)
    low, high = shift(low, "z", -1), shift(high, "z", 1)
    p1, p3 = attend(core[None], (q1, q3), near, far)
    low, high, p1, p3 = after(low, high, p1, p3)
    s1 = jnp.concatenate([add(out1[:32], low), out1[32:]], axis=0)
    s3 = jnp.concatenate([out3[:32], add(out3[32:], high)], axis=0)
    s1, s3, q2, again = after(s1, s3, q2, query)
    r1, r3 = shift(s1, "z", -1), shift(s3, "z", 1)
    v1, v3 = shift(p1, "y", -1), shift(p3, "y", 1)
    p2, p0 = attend(core[None], (q2, again), near, far)
    r1, r3, p2, p0, v1, v3 = after(r1, r3, p2, p0, v1, v3)
    v2 = shift(p2, "y", 2)
    own = add(out0, r1, r3).reshape(16, 4, D)
    moe = lax.all_to_all(own, "seq", 0, 0, tiled=True)
    moe = jnp.sum(moe.astype(f32), axis=0).astype(bf16)
    attn = merge(query, own_latent, [p0, v1, v2, v3]).reshape(4, 64, LAT)
    return attn, moe


def solution(mesh):
    in_specs = (
        P(AXES, None, None),
        P(AXES, None),
        P(None, "seq", None),
        P(AXES),
        P(AXES, None),
        P(AXES, None),
        P(AXES, None),
        P("exp", None, "seq"),
        P("exp", None, "seq"),
        P("exp", "seq", None),
    )
    out_specs = (P(AXES, None, None), P(AXES, None))
    return jax.shard_map(body, mesh=mesh, in_specs=in_specs, out_specs=out_specs, check_vma=False)
```

```python
import math

import jax
import jax.numpy as jnp
from jax import lax
from jax.experimental import pallas as pl
from jax.experimental.pallas import tpu as pltpu
from jax.sharding import PartitionSpec as P

LAT = 512
KDIM = 576
QW = 640
D = 7168
XW = D + 128
KC = 2560
SCALE2 = 192.0 ** (-0.5) * math.log2(math.e)
AXES = ("seq", "exp")
bf16 = jnp.bfloat16
f32 = jnp.float32


def shift(a, axis, s):
    pairs = []
    for y in range(4):
        for x in range(4):
            for z in range(4):
                for c in range(2):
                    to = dict(y=y, x=x, z=z, c=c)
                    to[axis] = (to[axis] + s) % (2 if axis == "c" else 4)
                    src = ((y * 4 + x) * 4 + z) * 2 + c
                    dst = ((to["y"] * 4 + to["x"]) * 4 + to["z"]) * 2 + to["c"]
                    pairs.append((src, dst))
    return lax.ppermute(a, AXES, pairs)


def after(*arrays):
    return lax.optimization_barrier(arrays)


def add(*parts):
    out = parts[0].astype(f32)
    for p in parts[1:]:
        out = out + p.astype(f32)
    return out.astype(bf16)


def in_hbm(*arrays):
    return [pltpu.with_memory_space_constraint(a, pltpu.HBM) for a in arrays]


def attend_kernel(core_ref, *refs):
    qs, own, near, far, outs = refs[0:2], refs[2], refs[3], refs[4], refs[5:7]
    q_ref, k_ref, s_ref, o_ref, sems = refs[7:12]
    core = core_ref[0]
    coref = core.astype(f32)
    cps = []

    def load(src, dst):
        cps.append(pltpu.make_async_copy(src, dst, sems.at[len(cps) + 2]))

    load(qs[0], q_ref.at[0])
    load(qs[1], q_ref.at[1])
    for g, (mine, got) in enumerate(((own.at[core], near), (own.at[1 - core], far))):
        load(mine, k_ref.at[g, 0])
        load(got, k_ref.at[g, 1:4])
    for cp in cps:
        cp.start()
    for cp in cps:
        cp.wait()
    lane = lax.broadcasted_iota(jnp.int32, (256, QW - LAT), 1)
    stores = []
    for step in range(2):
        q = q_ref[step, :, 0:KDIM]
        is_a = q_ref[step, :, KDIM : KDIM + 1].astype(f32) == coref
        best = []
        for g in range(2):
            m = None
            for t in range(4):
                s = jnp.dot(q, k_ref[g, t], preferred_element_type=f32)
                s_ref[g * 4 + t] = s
                ms = jnp.max(s, axis=1, keepdims=True)
                m = ms if m is None else jnp.maximum(m, ms)
            best.append(m)
        mu = jnp.where(is_a, best[0], best[1]) * SCALE2
        hi = mu.astype(bf16).astype(f32)
        lo = (mu - hi).astype(bf16).astype(f32)
        top = hi + lo
        total = jnp.zeros((256, 1), f32)
        acc = jnp.zeros((256, LAT), f32)
        for g in range(2):
            off = jnp.where(is_a if g == 0 else jnp.logical_not(is_a), -top, -1e30)
            for t in range(4):
                w = jnp.exp2(s_ref[g * 4 + t] * SCALE2 + off).astype(bf16)
                total = total + jnp.sum(w.astype(f32), axis=1, keepdims=True)
                acc = acc + lax.dot_general(
                    w,
                    k_ref[g, t, 0:LAT, :],
                    (((1,), (1,)), ((), ())),
                    preferred_element_type=f32,
                )
        o_ref[step, :, 0:LAT] = acc.astype(bf16)
        l_hi = total.astype(bf16).astype(f32)
        l_lo = total - l_hi
        tail = jnp.where(
            lane == 0,
            hi,
            jnp.where(lane == 1, lo, jnp.where(lane == 2, l_hi, jnp.where(lane == 3, l_lo, 0.0))),
        )
        o_ref[step, :, LAT:QW] = tail.astype(bf16)
        cp = pltpu.make_async_copy(o_ref.at[step], outs[step], sems.at[step])
        cp.start()
        stores.append(cp)
    for cp in stores:
        cp.wait()


def attend(core, qs, own, near, far):
    hbm = pl.BlockSpec(memory_space=pltpu.HBM)
    return pl.pallas_call(
        attend_kernel,
        out_shape=[pltpu.HBM((256, QW), bf16)] * 2,
        in_specs=[pl.BlockSpec(memory_space=pltpu.SMEM)] + [hbm] * 5,
        out_specs=[hbm] * 2,
        scratch_shapes=[
            pltpu.VMEM((2, 256, QW), bf16),
            pltpu.VMEM((2, 4, KDIM, 512), bf16),
            pltpu.VMEM((8, 256, 512), f32),
            pltpu.VMEM((2, 256, QW), bf16),
            pltpu.SemaphoreType.DMA((8,)),
        ],
        compiler_params=pltpu.CompilerParams(vmem_limit_bytes=40 << 20),
        cost_estimate=pl.CostEstimate(
            flops=4_500_000_000, transcendentals=2_000_000, bytes_accessed=6_000_000
        ),
        name="attend",
    )(core, *in_hbm(*qs, own, near.reshape(3, KDIM, 512), far.reshape(3, KDIM, 512)))


def merge_kernel(q_ref, lat_ref, *refs):
    parts, out_ref = refs[0:4], refs[4]
    for leaf in range(4):
        r = slice(leaf * 64, leaf * 64 + 64)
        lat = lat_ref[leaf : leaf + 1, :].astype(f32)
        own = jnp.sum(q_ref[r, 0:KDIM].astype(f32) * lat, axis=1, keepdims=True) * SCALE2
        tails = [p[r, LAT:QW].astype(f32) for p in parts]
        tops = [t[:, 0:1] + t[:, 1:2] for t in tails]
        m = own
        for t in tops:
            m = jnp.maximum(m, t)
        w = jnp.exp2(own - m)
        num = w * lat[:, 0:LAT]
        den = w
        for p, t, top in zip(parts, tails, tops):
            w = jnp.exp2(top - m)
            num = num + w * p[r, 0:LAT].astype(f32)
            den = den + w * (t[:, 2:3] + t[:, 3:4])
        out_ref[r, :] = (num / den).astype(bf16)


def merge(q, lat, parts):
    vmem = pl.BlockSpec(memory_space=pltpu.VMEM)
    return pl.pallas_call(
        merge_kernel,
        out_shape=jax.ShapeDtypeStruct((256, LAT), bf16),
        in_specs=[vmem] * 6,
        out_specs=vmem,
        name="merge",
    )(q, lat, *parts)


def expert_kernel(e_ref, *refs):
    xs, (wg, wu, wd, wg2, wu2, wd2), outs = refs[0:5], refs[5:11], refs[11:16]
    x_ref, w_ref, d_ref, acc_ref, o_ref, sems = refs[16:22]
    bounds = [(k, min(k + KC, D)) for k in range(0, D, KC)]
    count = [0]

    def copy(src, dst):
        cp = pltpu.make_async_copy(src, dst, sems.at[count[0]])
        count[0] += 1
        cp.start()
        return cp

    steps = []
    for k0, k1 in bounds:
        cps = []
        for j, w in enumerate((wg, wu, wg2, wu2)):
            cps.append(copy(w.at[k0:k1, :], w_ref.at[k0:k1, j * 128 : j * 128 + 128]))
        end = XW if k1 == D else k1
        r = 0
        for x in xs:
            cps.append(copy(x.at[:, k0:end], x_ref.at[r : r + x.shape[0], k0:end]))
            r += x.shape[0]
        steps.append(cps)
    down = [copy(wd, d_ref.at[0:128, :]), copy(wd2, d_ref.at[128:256, :])]
    for i, (k0, k1) in enumerate(bounds):
        for cp in steps[i]:
            cp.wait()
        part = jnp.dot(x_ref[:, k0:k1], w_ref[k0:k1, :], preferred_element_type=f32)
        if i == 0:
            acc_ref[...] = part
        else:
            acc_ref[...] += part
    gates = x_ref[:, D:XW].astype(f32)
    lane = lax.broadcasted_iota(jnp.int32, (256, 128), 1)
    halves = []
    for j in range(2):
        e = e_ref[j]
        pick = jnp.logical_or(lane == e, lane == e + 8)
        weight = jnp.sum(jnp.where(pick, gates, 0.0), axis=1, keepdims=True)
        g = acc_ref[:, j * 256 : j * 256 + 128]
        u = acc_ref[:, j * 256 + 128 : j * 256 + 256]
        halves.append((g / (1.0 + jnp.exp(-g)) * u * weight).astype(bf16))
    hidden = jnp.concatenate(halves, axis=1)
    for cp in down:
        cp.wait()
    stores = []
    for n in range(0, D, 1024):
        y = jnp.dot(hidden, d_ref[:, n : n + 1024], preferred_element_type=f32)
        o_ref[:, n : n + 1024] = y.astype(bf16)
        r = 0
        for out in outs:
            stores.append(
                copy(o_ref.at[r : r + out.shape[0], n : n + 1024], out.at[:, n : n + 1024])
            )
            r += out.shape[0]
    for cp in stores:
        cp.wait()


def experts(e, xs, weights):
    hbm = pl.BlockSpec(memory_space=pltpu.HBM)
    return pl.pallas_call(
        expert_kernel,
        out_shape=[pltpu.HBM((n, D), bf16) for n in (64, 64, 32, 32, 64)],
        in_specs=[pl.BlockSpec(memory_space=pltpu.SMEM)] + [hbm] * 11,
        out_specs=[hbm] * 5,
        scratch_shapes=[
            pltpu.VMEM((256, XW), bf16),
            pltpu.VMEM((D, 512), bf16),
            pltpu.VMEM((256, D), bf16),
            pltpu.VMEM((256, 512), f32),
            pltpu.VMEM((256, D), bf16),
            pltpu.SemaphoreType.DMA((72,)),
        ],
        compiler_params=pltpu.CompilerParams(vmem_limit_bytes=48 << 20),
        cost_estimate=pl.CostEstimate(
            flops=3_000_000_000, transcendentals=65_536, bytes_accessed=18_000_000
        ),
        name="experts",
    )(e, *in_hbm(*xs, *weights))


def body(
    queries,
    own_latent,
    snapshots,
    leaf_snapshot,
    moe_input,
    expert_ids,
    gate_weights,
    w_gate,
    w_up,
    w_down,
):
    place = lax.axis_index("exp").astype(jnp.int32)
    core = place & 1

    hit = (expert_ids[:, :, None] == jnp.arange(8, dtype=jnp.int32)).astype(f32)
    gate = jnp.sum(gate_weights[:, :, None] * hit, axis=1)
    high = lax.reduce_precision(gate, 8, 7)
    tail = jnp.concatenate([high, gate - high, jnp.zeros((4, 112), f32)], axis=1).astype(bf16)
    row = jnp.concatenate([moe_input, tail], axis=1)
    rows = lax.all_to_all(
        jnp.broadcast_to(row[None], (16, 4, XW)), "seq", 0, 0, tiled=True
    ).reshape(64, XW)
    weights = [w_gate[0], w_up[0], w_down[0]]
    other = [shift(w, "c", 1) for w in weights]

    choice = jnp.broadcast_to(leaf_snapshot.astype(bf16)[:, None, None], (4, 64, QW - KDIM))
    query = jnp.concatenate([queries, choice], axis=2).reshape(256, QW)
    keys = jnp.transpose(snapshots, (0, 2, 1))
    half = lax.dynamic_index_in_dim(keys, core, 0, keepdims=False)
    rows, half, query, *other = after(rows, half, query, *other)
    weights = weights + other

    z1, z3 = shift(rows, "z", 1), shift(rows, "z", 3)
    k1, k3, q1 = shift(half, "x", 1), shift(half, "x", 3), shift(query, "y", 1)
    z1, z3, k1, k3, q1, half, query = after(z1, z3, k1, k3, q1, half, query)
    xs = [rows, z1, shift(z1[:32], "z", 1), shift(z3[32:], "z", 3), z3]
    k2, q3, q2 = shift(half, "x", 2), shift(query, "y", 3), shift(query, "y", 2)
    xs, k2, q3 = after(xs, k2, q3)
    near = jnp.concatenate([k1, k2, k3], axis=0)
    far = shift(near, "c", 1)

    out0, out1, low, high, out3 = experts(jnp.stack([place, place ^ 1]), xs, weights)
    low, high = shift(low, "z", -1), shift(high, "z", 1)
    p1, p3 = attend(core[None], (q1, q3), keys, near, far)
    low, high, p1, p3 = after(low, high, p1, p3)
    s1 = jnp.concatenate([add(out1[:32], low), out1[32:]], axis=0)
    s3 = jnp.concatenate([out3[:32], add(out3[32:], high)], axis=0)
    s1, s3, q2, again = after(s1, s3, q2, query)
    r1, r3 = shift(s1, "z", -1), shift(s3, "z", 1)
    v1, v3 = shift(p1, "y", -1), shift(p3, "y", 1)
    p2, p0 = attend(core[None], (q2, again), keys, near, far)
    v2 = shift(p2, "y", 2)
    r1, r3, p0, v1, v3 = after(r1, r3, p0, v1, v3)
    r1, r3, v2 = after(r1, r3, v2)
    own = add(out0, r1, r3).reshape(16, 4, D)
    moe = lax.all_to_all(own, "seq", 0, 0, tiled=True)
    moe = jnp.sum(moe.astype(f32), axis=0).astype(bf16)
    attn = merge(query, own_latent, [p0, v1, v2, v3]).reshape(4, 64, LAT)
    return attn, moe


def solution(mesh):
    in_specs = (
        P(AXES, None, None),
        P(AXES, None),
        P(None, "seq", None),
        P(AXES),
        P(AXES, None),
        P(AXES, None),
        P(AXES, None),
        P("exp", None, "seq"),
        P("exp", None, "seq"),
        P("exp", "seq", None),
    )
    out_specs = (P(AXES, None, None), P(AXES, None))
    return jax.shard_map(body, mesh=mesh, in_specs=in_specs, out_specs=out_specs, check_vma=False)
```

```python
import functools
import math

import jax
import jax.numpy as jnp
from jax import lax
from jax.experimental import pallas as pl
from jax.experimental.pallas import tpu as pltpu
from jax.sharding import PartitionSpec as P

LAT = 512
KDIM = 576
QW = 640
D = 7168
XW = D + 128
KC = 1792
SCALE2 = 192.0 ** (-0.5) * math.log2(math.e)
AXES = ("seq", "exp")
bf16 = jnp.bfloat16
f32 = jnp.float32


def shift(a, axis, s):
    pairs = []
    for y in range(4):
        for x in range(4):
            for z in range(4):
                for c in range(2):
                    to = dict(y=y, x=x, z=z, c=c)
                    to[axis] = (to[axis] + s) % (2 if axis == "c" else 4)
                    src = ((y * 4 + x) * 4 + z) * 2 + c
                    dst = ((to["y"] * 4 + to["x"]) * 4 + to["z"]) * 2 + to["c"]
                    pairs.append((src, dst))
    return lax.ppermute(a, AXES, pairs)


def after(*arrays):
    return lax.optimization_barrier(arrays)


def add(*parts):
    out = parts[0].astype(f32)
    for p in parts[1:]:
        out = out + p.astype(f32)
    return out.astype(bf16)


def in_hbm(*arrays):
    return [pltpu.with_memory_space_constraint(a, pltpu.HBM) for a in arrays]


def attend_kernel(core_ref, *refs):
    qs, own, near, far, outs = refs[0:2], refs[2], refs[3:6], refs[6:8], refs[8:10]
    q_ref, k_ref, s_ref, o_ref, sems = refs[10:15]
    core = core_ref[0]
    coref = core.astype(f32)
    cps = []

    def load(src, dst):
        cps.append(pltpu.make_async_copy(src, dst, sems.at[len(cps) + 2]))

    load(qs[0], q_ref.at[0:256])
    load(qs[1], q_ref.at[256:512])
    load(own.at[core], k_ref.at[0, 0])
    for i in range(3):
        load(near[i], k_ref.at[0, i + 1])
    load(own.at[1 - core], k_ref.at[1, 0])
    load(far[0], k_ref.at[1, 1:3])
    load(far[1], k_ref.at[1, 3])
    for cp in cps:
        cp.start()
    cps[0].wait()
    cps[1].wait()
    needs = [(2, 6), (3, 7), (4,), (5, 8)]
    lane = lax.broadcasted_iota(jnp.int32, (512, QW - LAT), 1)
    stores = []
    q = q_ref[:, 0:KDIM]
    is_a = q_ref[:, KDIM : KDIM + 1].astype(f32) == coref
    in_a = jnp.where(is_a, 1.0, 0.0).astype(bf16)
    in_b = jnp.where(is_a, 0.0, 1.0).astype(bf16)
    best = None
    for t in range(4):
        for i in needs[t]:
            cps[i].wait()
        sa = jnp.dot(q, k_ref[0, t], preferred_element_type=f32)
        sb = jnp.dot(q, k_ref[1, t], preferred_element_type=f32)
        s = jnp.where(is_a, sa, sb)
        s_ref[t] = s
        m = jnp.max(s, axis=1, keepdims=True)
        best = m if best is None else jnp.maximum(best, m)
    mu = best * SCALE2
    hi = mu.astype(bf16).astype(f32)
    lo = (mu - hi).astype(bf16).astype(f32)
    top = hi + lo
    total = jnp.zeros((512, 1), f32)
    acc = jnp.zeros((512, LAT), f32)
    for t in range(4):
        w = jnp.exp2(s_ref[t] * SCALE2 - top).astype(bf16)
        total = total + jnp.sum(w.astype(f32), axis=1, keepdims=True)
        for g, mask in enumerate((in_a, in_b)):
            acc = acc + lax.dot_general(
                w * mask,
                k_ref[g, t, 0:LAT, :],
                (((1,), (1,)), ((), ())),
                preferred_element_type=f32,
            )
    o_ref[:, 0:LAT] = acc.astype(bf16)
    l_hi = total.astype(bf16).astype(f32)
    l_lo = total - l_hi
    tail = jnp.where(
        lane == 0,
        hi,
        jnp.where(lane == 1, lo, jnp.where(lane == 2, l_hi, jnp.where(lane == 3, l_lo, 0.0))),
    )
    o_ref[:, LAT:QW] = tail.astype(bf16)
    for i in range(2):
        cp = pltpu.make_async_copy(o_ref.at[i * 256 : i * 256 + 256], outs[i], sems.at[i])
        cp.start()
        stores.append(cp)
    for cp in stores:
        cp.wait()


def attend(core, qs, own, near, far):
    hbm = pl.BlockSpec(memory_space=pltpu.HBM)
    return pl.pallas_call(
        attend_kernel,
        out_shape=[pltpu.HBM((256, QW), bf16)] * 2,
        in_specs=[pl.BlockSpec(memory_space=pltpu.SMEM)] + [hbm] * 8,
        out_specs=[hbm] * 2,
        scratch_shapes=[
            pltpu.VMEM((512, QW), bf16),
            pltpu.VMEM((2, 4, KDIM, 512), bf16),
            pltpu.VMEM((4, 512, 512), f32),
            pltpu.VMEM((512, QW), bf16),
            pltpu.SemaphoreType.DMA((11,)),
        ],
        compiler_params=pltpu.CompilerParams(vmem_limit_bytes=40 << 20),
        cost_estimate=pl.CostEstimate(
            flops=4_500_000_000, transcendentals=2_000_000, bytes_accessed=6_000_000
        ),
        name="attend",
    )(core, *in_hbm(*qs, own, *near, *far))


def merge_kernel(q_ref, lat_ref, *refs):
    parts, out_ref = refs[0:4], refs[4]
    for leaf in range(4):
        r = slice(leaf * 64, leaf * 64 + 64)
        lat = lat_ref[leaf : leaf + 1, :].astype(f32)
        own = jnp.sum(q_ref[r, 0:KDIM].astype(f32) * lat, axis=1, keepdims=True) * SCALE2
        tails = [p[r, LAT:QW].astype(f32) for p in parts]
        tops = [t[:, 0:1] + t[:, 1:2] for t in tails]
        m = own
        for t in tops:
            m = jnp.maximum(m, t)
        w = jnp.exp2(own - m)
        num = w * lat[:, 0:LAT]
        den = w
        for p, t, top in zip(parts, tails, tops):
            w = jnp.exp2(top - m)
            num = num + w * p[r, 0:LAT].astype(f32)
            den = den + w * (t[:, 2:3] + t[:, 3:4])
        out_ref[r, :] = (num / den).astype(bf16)


def merge(q, lat, parts):
    vmem = pl.BlockSpec(memory_space=pltpu.VMEM)
    return pl.pallas_call(
        merge_kernel,
        out_shape=jax.ShapeDtypeStruct((256, LAT), bf16),
        in_specs=[vmem] * 6,
        out_specs=vmem,
        name="merge",
    )(q, lat, *parts)


def expert_kernel(e_ref, *refs, count_x, fresh):
    xs, refs = refs[:count_x], refs[count_x:]
    if fresh:
        (wg, wu, wd, wg2, wu2, wd2), refs = refs[:6], refs[6:]
    else:
        (w_ref, d_ref), refs = refs[:2], refs[2:]
    outs, refs = refs[:count_x], refs[count_x:]
    if fresh:
        (w_ref, d_ref), refs = refs[:2], refs[2:]
    x_ref, acc_ref, o_ref, sems = refs
    height = x_ref.shape[0]
    bounds = [(k, min(k + KC, D)) for k in range(0, D, KC)]
    count = [0]

    def copy(src, dst):
        cp = pltpu.make_async_copy(src, dst, sems.at[count[0]])
        count[0] += 1
        cp.start()
        return cp

    steps = []
    for k0, k1 in bounds:
        cps = []
        if fresh:
            for j, w in enumerate((wg, wu, wg2, wu2)):
                cps.append(copy(w.at[k0:k1, :], w_ref.at[k0:k1, j * 128 : j * 128 + 128]))
        end = XW if k1 == D else k1
        r = 0
        for x in xs:
            cps.append(copy(x.at[:, k0:end], x_ref.at[r : r + x.shape[0], k0:end]))
            r += x.shape[0]
        steps.append(cps)
    down = []
    if fresh:
        down = [copy(wd, d_ref.at[0:128, :]), copy(wd2, d_ref.at[128:256, :])]
    for i, (k0, k1) in enumerate(bounds):
        for cp in steps[i]:
            cp.wait()
        part = jnp.dot(x_ref[:, k0:k1], w_ref[k0:k1, :], preferred_element_type=f32)
        if i == 0:
            acc_ref[...] = part
        else:
            acc_ref[...] += part
    gates = x_ref[:, D:XW].astype(f32)
    lane = lax.broadcasted_iota(jnp.int32, (height, 128), 1)
    halves = []
    for j in range(2):
        e = e_ref[j]
        pick = jnp.logical_or(lane == e, lane == e + 8)
        weight = jnp.sum(jnp.where(pick, gates, 0.0), axis=1, keepdims=True)
        g = acc_ref[:, j * 256 : j * 256 + 128]
        u = acc_ref[:, j * 256 + 128 : j * 256 + 256]
        halves.append((g / (1.0 + jnp.exp(-g)) * u * weight).astype(bf16))
    hidden = jnp.concatenate(halves, axis=1)
    for cp in down:
        cp.wait()
    stores = []
    for n in range(0, D, 1024):
        y = jnp.dot(hidden, d_ref[:, n : n + 1024], preferred_element_type=f32)
        o_ref[:, n : n + 1024] = y.astype(bf16)
        r = 0
        for out in outs:
            stores.append(
                copy(o_ref.at[r : r + out.shape[0], n : n + 1024], out.at[:, n : n + 1024])
            )
            r += out.shape[0]
    for cp in stores:
        cp.wait()


def experts(e, xs, weights, fresh):
    hbm = pl.BlockSpec(memory_space=pltpu.HBM)
    vmem = pl.BlockSpec(memory_space=pltpu.VMEM)
    height = sum(x.shape[0] for x in xs)
    out_shape = [pltpu.HBM((x.shape[0], D), bf16) for x in xs]
    if fresh:
        out_shape += [pltpu.VMEM((D, 512), bf16), pltpu.VMEM((256, D), bf16)]
        weights = in_hbm(*weights)
    else:
        weights = [pltpu.with_memory_space_constraint(w, pltpu.VMEM) for w in weights]
    return pl.pallas_call(
        functools.partial(expert_kernel, count_x=len(xs), fresh=fresh),
        out_shape=out_shape,
        in_specs=[pl.BlockSpec(memory_space=pltpu.SMEM)]
        + [hbm] * len(xs)
        + [hbm if fresh else vmem] * len(weights),
        out_specs=[hbm] * len(xs) + [vmem, vmem] * fresh,
        scratch_shapes=[
            pltpu.VMEM((height, XW), bf16),
            pltpu.VMEM((height, 512), f32),
            pltpu.VMEM((height, D), bf16),
            pltpu.SemaphoreType.DMA((72,)),
        ],
        compiler_params=pltpu.CompilerParams(vmem_limit_bytes=32 << 20),
        cost_estimate=pl.CostEstimate(
            flops=11_000_000 * height,
            transcendentals=256 * height,
            bytes_accessed=11_000_000 * fresh + 30_000 * height,
        ),
        name="experts",
    )(e, *in_hbm(*xs), *weights)


def body(
    queries,
    own_latent,
    snapshots,
    leaf_snapshot,
    moe_input,
    expert_ids,
    gate_weights,
    w_gate,
    w_up,
    w_down,
):
    place = lax.axis_index("exp").astype(jnp.int32)
    core = place & 1

    hit = (expert_ids[:, :, None] == jnp.arange(8, dtype=jnp.int32)).astype(f32)
    gate = jnp.sum(gate_weights[:, :, None] * hit, axis=1)
    high = lax.reduce_precision(gate, 8, 7)
    tail = jnp.concatenate([high, gate - high, jnp.zeros((4, 112), f32)], axis=1).astype(bf16)
    row = jnp.concatenate([moe_input, tail], axis=1)
    rows = lax.all_to_all(
        jnp.broadcast_to(row[None], (16, 4, XW)), "seq", 0, 0, tiled=True
    ).reshape(64, XW)
    weights = [w_gate[0], w_up[0], w_down[0]]
    other = [shift(w, "c", 1) for w in weights]

    choice = jnp.broadcast_to(leaf_snapshot.astype(bf16)[:, None, None], (4, 64, QW - KDIM))
    query = jnp.concatenate([queries, choice], axis=2).reshape(256, QW)
    keys = jnp.transpose(snapshots, (0, 2, 1))
    half = lax.dynamic_index_in_dim(keys, core, 0, keepdims=False)
    rows, half, query, *other = after(rows, half, query, *other)
    weights = weights + other

    z1, z3 = shift(rows, "z", 1), shift(rows, "z", 3)
    k1, k3, q1 = shift(half, "x", 1), shift(half, "x", 3), shift(query, "y", 1)
    k1, k3, q1, half, query = after(k1, k3, q1, half, query)
    mine = [rows, z1, z3]
    last = [shift(z1[:32], "z", 1), shift(z3[32:], "z", 3)]
    k2, q3, q2 = shift(half, "x", 2), shift(query, "y", 3), shift(query, "y", 2)
    far = shift(jnp.stack([k1, k3]), "c", 1)
    near = [k1, k3, k2]
    numbers = jnp.stack([place, place ^ 1])
    *mine, w_all, d_all = experts(numbers, mine, weights, True)
    last, mine, k2, q3, far = after(last, mine, k2, q3, far)
    far = [far, shift(k2, "c", 1)]
    out0, out1, out3 = mine
    low, high = experts(numbers, last, [w_all, d_all], False)
    low, high = shift(low, "z", -1), shift(high, "z", 1)
    p1, p3 = attend(core[None], (q1, q3), keys, near, far)
    low, high, p1, p3 = after(low, high, p1, p3)
    s1 = add(out1, jnp.pad(low, ((0, 32), (0, 0))))
    s3 = add(out3, jnp.pad(high, ((32, 0), (0, 0))))
    s1, s3, q2, again = after(s1, s3, q2, query)
    r1, r3 = shift(s1, "z", -1), shift(s3, "z", 1)
    v1, v3 = shift(p1, "y", -1), shift(p3, "y", 1)
    p2, p0 = attend(core[None], (q2, again), keys, near, far)
    v2 = shift(p2, "y", 2)
    r1, r3, p0, v1, v3 = after(r1, r3, p0, v1, v3)
    r1, r3, v2 = after(r1, r3, v2)
    own = add(out0, r1, r3).reshape(16, 4, D)
    moe = lax.all_to_all(own, "seq", 0, 0, tiled=True)
    moe = jnp.sum(moe.astype(f32), axis=0).astype(bf16)
    attn = merge(query, own_latent, [p0, v1, v2, v3]).reshape(4, 64, LAT)
    return attn, moe


def solution(mesh):
    in_specs = (
        P(AXES, None, None),
        P(AXES, None),
        P(None, "seq", None),
        P(AXES),
        P(AXES, None),
        P(AXES, None),
        P(AXES, None),
        P("exp", None, "seq"),
        P("exp", None, "seq"),
        P("exp", "seq", None),
    )
    out_specs = (P(AXES, None, None), P(AXES, None))
    return jax.shard_map(body, mesh=mesh, in_specs=in_specs, out_specs=out_specs, check_vma=False)
```

```python
import functools
import math

import jax
import jax.numpy as jnp
from jax import lax
from jax.experimental import pallas as pl
from jax.experimental.pallas import tpu as pltpu
from jax.sharding import PartitionSpec as P

LAT = 512
KDIM = 576
QW = 640
D = 7168
XW = D + 128
KC = 1024
SCALE2 = 192.0 ** (-0.5) * math.log2(math.e)
AXES = ("seq", "exp")
bf16 = jnp.bfloat16
f32 = jnp.float32


def shift(a, axis, s):
    pairs = []
    for y in range(4):
        for x in range(4):
            for z in range(4):
                for c in range(2):
                    to = dict(y=y, x=x, z=z, c=c)
                    to[axis] = (to[axis] + s) % (2 if axis == "c" else 4)
                    src = ((y * 4 + x) * 4 + z) * 2 + c
                    dst = ((to["y"] * 4 + to["x"]) * 4 + to["z"]) * 2 + to["c"]
                    pairs.append((src, dst))
    return lax.ppermute(a, AXES, pairs)


def after(*arrays):
    return lax.optimization_barrier(arrays)


def add(*parts):
    out = parts[0].astype(f32)
    for p in parts[1:]:
        out = out + p.astype(f32)
    return out.astype(bf16)


def in_hbm(*arrays):
    return [pltpu.with_memory_space_constraint(a, pltpu.HBM) for a in arrays]


def attend_kernel(core_ref, *refs):
    qs, own, near, far, outs = refs[0:2], refs[2], refs[3:6], refs[6:8], refs[8:10]
    q_ref, k_ref, s_ref, o_ref, sems = refs[10:15]
    core = core_ref[0]
    coref = core.astype(f32)
    cps = []

    def load(src, dst):
        cps.append(pltpu.make_async_copy(src, dst, sems.at[len(cps) + 2]))

    load(qs[0], q_ref.at[0:256])
    load(qs[1], q_ref.at[256:512])
    load(own.at[core], k_ref.at[0, 0])
    for i in range(3):
        load(near[i], k_ref.at[0, i + 1])
    load(own.at[1 - core], k_ref.at[1, 0])
    load(far[0], k_ref.at[1, 1:3])
    load(far[1], k_ref.at[1, 3])
    for cp in cps:
        cp.start()
    cps[0].wait()
    cps[1].wait()
    needs = [(2, 6), (3, 7), (4,), (5, 8)]
    lane = lax.broadcasted_iota(jnp.int32, (512, QW - LAT), 1)
    stores = []
    q = q_ref[:, 0:KDIM]
    is_a = q_ref[:, KDIM : KDIM + 1].astype(f32) == coref
    in_a = jnp.where(is_a, 1.0, 0.0).astype(bf16)
    in_b = jnp.where(is_a, 0.0, 1.0).astype(bf16)
    best = None
    for t in range(4):
        for i in needs[t]:
            cps[i].wait()
        sa = jnp.dot(q, k_ref[0, t], preferred_element_type=f32)
        sb = jnp.dot(q, k_ref[1, t], preferred_element_type=f32)
        s = jnp.where(is_a, sa, sb)
        s_ref[t] = s
        m = jnp.max(s, axis=1, keepdims=True)
        best = m if best is None else jnp.maximum(best, m)
    mu = best * SCALE2
    hi = mu.astype(bf16).astype(f32)
    lo = (mu - hi).astype(bf16).astype(f32)
    top = hi + lo
    total = jnp.zeros((512, 1), f32)
    acc = jnp.zeros((512, LAT), f32)
    for t in range(4):
        w = jnp.exp2(s_ref[t] * SCALE2 - top).astype(bf16)
        total = total + jnp.sum(w.astype(f32), axis=1, keepdims=True)
        for g, mask in enumerate((in_a, in_b)):
            acc = acc + lax.dot_general(
                w * mask,
                k_ref[g, t, 0:LAT, :],
                (((1,), (1,)), ((), ())),
                preferred_element_type=f32,
            )
    o_ref[:, 0:LAT] = acc.astype(bf16)
    l_hi = total.astype(bf16).astype(f32)
    l_lo = total - l_hi
    tail = jnp.where(
        lane == 0,
        hi,
        jnp.where(lane == 1, lo, jnp.where(lane == 2, l_hi, jnp.where(lane == 3, l_lo, 0.0))),
    )
    o_ref[:, LAT:QW] = tail.astype(bf16)
    for i in range(2):
        cp = pltpu.make_async_copy(o_ref.at[i * 256 : i * 256 + 256], outs[i], sems.at[i])
        cp.start()
        stores.append(cp)
    for cp in stores:
        cp.wait()


def attend(core, qs, own, near, far):
    hbm = pl.BlockSpec(memory_space=pltpu.HBM)
    return pl.pallas_call(
        attend_kernel,
        out_shape=[pltpu.HBM((256, QW), bf16)] * 2,
        in_specs=[pl.BlockSpec(memory_space=pltpu.SMEM)] + [hbm] * 8,
        out_specs=[hbm] * 2,
        scratch_shapes=[
            pltpu.VMEM((512, QW), bf16),
            pltpu.VMEM((2, 4, KDIM, 512), bf16),
            pltpu.VMEM((4, 512, 512), f32),
            pltpu.VMEM((512, QW), bf16),
            pltpu.SemaphoreType.DMA((11,)),
        ],
        compiler_params=pltpu.CompilerParams(vmem_limit_bytes=40 << 20),
        cost_estimate=pl.CostEstimate(
            flops=4_500_000_000, transcendentals=2_000_000, bytes_accessed=6_000_000
        ),
        name="attend",
    )(core, *in_hbm(*qs, own, *near, *far))


def merge_kernel(q_ref, lat_ref, *refs):
    parts, out_ref = refs[0:4], refs[4]
    for leaf in range(4):
        r = slice(leaf * 64, leaf * 64 + 64)
        lat = lat_ref[leaf : leaf + 1, :].astype(f32)
        own = jnp.sum(q_ref[r, 0:KDIM].astype(f32) * lat, axis=1, keepdims=True) * SCALE2
        tails = [p[r, LAT:QW].astype(f32) for p in parts]
        tops = [t[:, 0:1] + t[:, 1:2] for t in tails]
        m = own
        for t in tops:
            m = jnp.maximum(m, t)
        w = jnp.exp2(own - m)
        num = w * lat[:, 0:LAT]
        den = w
        for p, t, top in zip(parts, tails, tops):
            w = jnp.exp2(top - m)
            num = num + w * p[r, 0:LAT].astype(f32)
            den = den + w * (t[:, 2:3] + t[:, 3:4])
        out_ref[r, :] = (num / den).astype(bf16)


def merge(q, lat, parts):
    vmem = pl.BlockSpec(memory_space=pltpu.VMEM)
    return pl.pallas_call(
        merge_kernel,
        out_shape=jax.ShapeDtypeStruct((256, LAT), bf16),
        in_specs=[vmem] * 6,
        out_specs=vmem,
        name="merge",
    )(q, lat, *parts)


def expert_kernel(e_ref, *refs, count_x, fresh):
    xs, refs = refs[:count_x], refs[count_x:]
    if fresh:
        (wg, wu, wd, wg2, wu2, wd2), refs = refs[:6], refs[6:]
    else:
        (w_ref, d_ref), refs = refs[:2], refs[2:]
    outs, refs = refs[:count_x], refs[count_x:]
    if fresh:
        (w_ref, d_ref), refs = refs[:2], refs[2:]
    x_ref, acc_ref, o_ref, sems = refs
    height = x_ref.shape[0]
    bounds = [(k, min(k + KC, D)) for k in range(0, D, KC)]
    count = [0]

    def copy(src, dst):
        cp = pltpu.make_async_copy(src, dst, sems.at[count[0]])
        count[0] += 1
        cp.start()
        return cp

    steps = []
    for k0, k1 in bounds:
        cps = []
        if fresh:
            for j, w in enumerate((wg, wu, wg2, wu2)):
                cps.append(copy(w.at[k0:k1, :], w_ref.at[k0:k1, j * 128 : j * 128 + 128]))
        end = XW if k1 == D else k1
        r = 0
        for x in xs:
            cps.append(copy(x.at[:, k0:end], x_ref.at[r : r + x.shape[0], k0:end]))
            r += x.shape[0]
        steps.append(cps)
    down = []
    if fresh:
        down = [copy(wd, d_ref.at[0:128, :]), copy(wd2, d_ref.at[128:256, :])]
    for i, (k0, k1) in enumerate(bounds):
        for cp in steps[i]:
            cp.wait()
        part = jnp.dot(x_ref[:, k0:k1], w_ref[k0:k1, :], preferred_element_type=f32)
        if i == 0:
            acc_ref[...] = part
        else:
            acc_ref[...] += part
    gates = x_ref[:, D:XW].astype(f32)
    lane = lax.broadcasted_iota(jnp.int32, (height, 128), 1)
    halves = []
    for j in range(2):
        e = e_ref[j]
        pick = jnp.logical_or(lane == e, lane == e + 8)
        weight = jnp.sum(jnp.where(pick, gates, 0.0), axis=1, keepdims=True)
        g = acc_ref[:, j * 256 : j * 256 + 128]
        u = acc_ref[:, j * 256 + 128 : j * 256 + 256]
        halves.append((g / (1.0 + jnp.exp(-g)) * u * weight).astype(bf16))
    hidden = jnp.concatenate(halves, axis=1)
    for cp in down:
        cp.wait()
    stores = []
    for n in range(0, D, 1024):
        y = jnp.dot(hidden, d_ref[:, n : n + 1024], preferred_element_type=f32)
        o_ref[:, n : n + 1024] = y.astype(bf16)
        r = 0
        for out in outs:
            stores.append(
                copy(o_ref.at[r : r + out.shape[0], n : n + 1024], out.at[:, n : n + 1024])
            )
            r += out.shape[0]
    for cp in stores:
        cp.wait()


def experts(e, xs, weights, fresh):
    hbm = pl.BlockSpec(memory_space=pltpu.HBM)
    vmem = pl.BlockSpec(memory_space=pltpu.VMEM)
    height = sum(x.shape[0] for x in xs)
    out_shape = [pltpu.HBM((x.shape[0], D), bf16) for x in xs]
    if fresh:
        out_shape += [pltpu.VMEM((D, 512), bf16), pltpu.VMEM((256, D), bf16)]
        weights = in_hbm(*weights)
    else:
        weights = [pltpu.with_memory_space_constraint(w, pltpu.VMEM) for w in weights]
    return pl.pallas_call(
        functools.partial(expert_kernel, count_x=len(xs), fresh=fresh),
        out_shape=out_shape,
        in_specs=[pl.BlockSpec(memory_space=pltpu.SMEM)]
        + [hbm] * len(xs)
        + [hbm if fresh else vmem] * len(weights),
        out_specs=[hbm] * len(xs) + [vmem, vmem] * fresh,
        scratch_shapes=[
            pltpu.VMEM((height, XW), bf16),
            pltpu.VMEM((height, 512), f32),
            pltpu.VMEM((height, D), bf16),
            pltpu.SemaphoreType.DMA((80,)),
        ],
        compiler_params=pltpu.CompilerParams(vmem_limit_bytes=32 << 20),
        cost_estimate=pl.CostEstimate(
            flops=11_000_000 * height,
            transcendentals=256 * height,
            bytes_accessed=11_000_000 * fresh + 30_000 * height,
        ),
        name="experts",
    )(e, *in_hbm(*xs), *weights)


def body(
    queries,
    own_latent,
    snapshots,
    leaf_snapshot,
    moe_input,
    expert_ids,
    gate_weights,
    w_gate,
    w_up,
    w_down,
):
    place = lax.axis_index("exp").astype(jnp.int32)
    core = place & 1

    hit = (expert_ids[:, :, None] == jnp.arange(8, dtype=jnp.int32)).astype(f32)
    gate = jnp.sum(gate_weights[:, :, None] * hit, axis=1)
    high = lax.reduce_precision(gate, 8, 7)
    tail = jnp.concatenate([high, gate - high, jnp.zeros((4, 112), f32)], axis=1).astype(bf16)
    row = jnp.concatenate([moe_input, tail], axis=1)
    rows = lax.all_to_all(
        jnp.broadcast_to(row[None], (16, 4, XW)), "seq", 0, 0, tiled=True
    ).reshape(64, XW)
    weights = [w_gate[0], w_up[0], w_down[0]]
    other = [shift(w, "c", 1) for w in weights]

    choice = jnp.broadcast_to(leaf_snapshot.astype(bf16)[:, None, None], (4, 64, QW - KDIM))
    query = jnp.concatenate([queries, choice], axis=2).reshape(256, QW)
    keys = jnp.transpose(snapshots, (0, 2, 1))
    half = lax.dynamic_index_in_dim(keys, core, 0, keepdims=False)
    rows, half, query, *other = after(rows, half, query, *other)
    weights = weights + other

    z1, z3 = shift(rows, "z", 1), shift(rows, "z", 3)
    k1, k3, q1 = shift(half, "x", 1), shift(half, "x", 3), shift(query, "y", 1)
    k1, k3, q1, half, query = after(k1, k3, q1, half, query)
    mine = [rows, z1, z3]
    last = [shift(z1[:32], "z", 1), shift(z3[32:], "z", 3)]
    k2, q3, q2 = shift(half, "x", 2), shift(query, "y", 3), shift(query, "y", 2)
    far = shift(jnp.stack([k1, k3]), "c", 1)
    near = [k1, k3, k2]
    numbers = jnp.stack([place, place ^ 1])
    *mine, w_all, d_all = experts(numbers, mine, weights, True)
    last, mine, k2, q3, far = after(last, mine, k2, q3, far)
    far = [far, shift(k2, "c", 1)]
    out0, out1, out3 = mine
    low, high = experts(numbers, last, [w_all, d_all], False)
    low, high = shift(low, "z", -1), shift(high, "z", 1)
    p1, p3 = attend(core[None], (q1, q3), keys, near, far)
    low, high, p1, p3 = after(low, high, p1, p3)
    s1 = add(out1, jnp.pad(low, ((0, 32), (0, 0))))
    s3 = add(out3, jnp.pad(high, ((32, 0), (0, 0))))
    s1, s3, q2, again = after(s1, s3, q2, query)
    r1, r3 = shift(s1, "z", -1), shift(s3, "z", 1)
    v1, v3 = shift(p1, "y", -1), shift(p3, "y", 1)
    p2, p0 = attend(core[None], (q2, again), keys, near, far)
    v2 = shift(p2, "y", 2)
    r1, r3, p0, v1, v3 = after(r1, r3, p0, v1, v3)
    r1, r3, v2 = after(r1, r3, v2)
    own = add(out0, r1, r3).reshape(16, 4, D)
    moe = lax.all_to_all(own, "seq", 0, 0, tiled=True)
    moe = jnp.sum(moe.astype(f32), axis=0).astype(bf16)
    attn = merge(query, own_latent, [p0, v1, v2, v3]).reshape(4, 64, LAT)
    return attn, moe


def solution(mesh):
    in_specs = (
        P(AXES, None, None),
        P(AXES, None),
        P(None, "seq", None),
        P(AXES),
        P(AXES, None),
        P(AXES, None),
        P(AXES, None),
        P("exp", None, "seq"),
        P("exp", None, "seq"),
        P("exp", "seq", None),
    )
    out_specs = (P(AXES, None, None), P(AXES, None))
    return jax.shard_map(body, mesh=mesh, in_specs=in_specs, out_specs=out_specs, check_vma=False)
```
